32 devices in a mesh: pb: 4 (over y, core), wa: 8 (over z, x).
Axes of the slice: x: 2, y: 2, z: 4, core: 2. Of those that a mesh axis runs over, the one named last changes fastest.
Arguments:
- state: float32 [2, 8388608], P(None, ('pb', 'wa')), may hold values from -6 to 6
- gate_bank: float32 [4, 2, 128, 128], replicated, may hold values from -0.375 to 0.375
- pass_order: int32 [4], replicated, may hold values from 0 to 3, each once
Outputs:
- evolved: float32 [2, 8388608], P(None, ('pb', 'wa'))
The draws below stay inside these ranges and needn't reach their ends.
Inputs may be any that keep to these rules, and one draw needn't show every extreme that they name: `pass_order`: each pass index 0 to 3 appears once.
All inputs are finite; a program needn't handle non-finite values.
Results may differ from the reference program's by a relative error of at most 0.0001.
Values sent between devices are 32-bit elements; how exact they have to be, the bound alone decides.
A program may use at most 64 MiB of HBM per device.

```python
import jax
import jax.numpy as jnp
from jax import lax

LQ = 18
GATE = 128
LAYERS = 2
PASSES = 4
AMPS = 8388608
N_PB = 4
N_WA = 8


def shard_levels(stream_key, dims, pieces, low, high):
    level = 1.0
    for axis_at, shards_of in pieces:
        draws = jax.random.uniform(jax.random.fold_in(jax.random.fold_in(stream_key, 6), axis_at), (shards_of,), jnp.float32, low / len(pieces), high / len(pieces))
        level = level * jnp.repeat(jnp.exp(draws), dims[axis_at] // shards_of).reshape((-1,) + (1,) * (len(dims) - 1 - axis_at))
    return level


def scatter_about(stream_key, dims, spread, bound, cuts=(), dtype=jnp.bfloat16):
    entries = spread * jax.random.normal(stream_key, dims, jnp.float32)
    if cuts:
        entries = entries * shard_levels(stream_key, dims, cuts, -0.22, 0.18)
    return jnp.clip(entries, -bound, bound).astype(dtype)


def setup_inputs(seed: int = 0) -> dict:
    arg_keys = jax.random.split(jax.random.key(seed), 4)
    return {
        "state": scatter_about(arg_keys[0], (2, AMPS), 1.0, 6.0, ((1, 32),), jnp.float32),
        "gate_bank": scatter_about(arg_keys[1], (PASSES, 2, GATE, GATE), (2 * GATE) ** -0.5, 0.375, (), jnp.float32),
        "pass_order": jax.random.permutation(arg_keys[2], PASSES).astype(jnp.int32),
    }


HIGH = lax.Precision.HIGHEST


def mix_left(gate, values):
    real = jnp.dot(gate[0], values[0], precision=HIGH) - jnp.dot(gate[1], values[1], precision=HIGH)
    imag = jnp.dot(gate[0], values[1], precision=HIGH) + jnp.dot(gate[1], values[0], precision=HIGH)
    return jnp.stack([real, imag])


def mix_right(gate, values):
    real = jnp.dot(values[0], gate[0].T, precision=HIGH) - jnp.dot(values[1], gate[1].T, precision=HIGH)
    imag = jnp.dot(values[1], gate[0].T, precision=HIGH) + jnp.dot(values[0], gate[1].T, precision=HIGH)
    return jnp.stack([real, imag])


def reference(state, gate_bank, pass_order):
    wa_bits = N_WA.bit_length() - 1
    middle = GATE // (2 * N_PB)
    rest = 2 ** LQ // GATE
    psi = state.astype(jnp.float32)
    for layer in range(LAYERS):
        first = gate_bank[pass_order[2 * layer]]
        psi = mix_right(first, psi.reshape(2, -1, GATE)).reshape(2, -1)
        second = gate_bank[pass_order[2 * layer + 1]]
        bit_pos = wa_bits - 1 if layer == 0 else 0
        low_wa = 2 ** bit_pos
        high_wa = N_WA // (2 * low_wa)
        shaped = psi.reshape(2, N_PB, high_wa, 2, low_wa, N_PB, 2, middle, rest)
        moved = jnp.transpose(shaped, (0, 1, 3, 7, 2, 4, 5, 6, 8))
        moved_shape = moved.shape
        mixed = mix_left(second, moved.reshape(2, GATE, -1)).reshape(moved_shape)
        psi = jnp.transpose(mixed, (0, 1, 4, 2, 5, 6, 7, 3, 8)).reshape(2, -1)
    return psi
```

```python
import functools

import jax
import jax.numpy as jnp
from jax import lax
from jax.experimental import pallas as pl
from jax.experimental.pallas import tpu as pltpu
from jax.sharding import PartitionSpec as P

MESH = pl.DeviceIdType.MESH
HIGH = lax.Precision.HIGHEST
CHUNKS = 2
SUB = 8


def dot(a, b):
    return lax.dot_general(
        a, b, (((1,), (0,)), ((), ())), precision=HIGH, preferred_element_type=jnp.float32
    )


def dot_t(a, b):
    return lax.dot_general(
        a, b, (((1,), (1,)), ((), ())), precision=HIGH, preferred_element_type=jnp.float32
    )


def embed(real, imag):
    upper = jnp.concatenate([real, -imag], axis=1)
    lower = jnp.concatenate([imag, real], axis=1)
    return jnp.concatenate([upper, lower], axis=0)


def spread_rows(groups, mid, gate_rows, high):
    slot = lax.broadcasted_iota(jnp.int32, (2 * gate_rows, gate_rows), 0)
    row = lax.broadcasted_iota(jnp.int32, (2 * gate_rows, gate_rows), 1)
    a = row // (2 * mid)
    w0 = (row // mid) % 2
    m = row % mid
    return jnp.where(slot == ((w0 * groups + a) * 2 + high) * mid + m, 1.0, 0.0).astype(jnp.float32)


def kernel(groups, wa_count, mid, order_ref, bank_ref, x_ref, out_ref, lanes_gate, rows_gate,
           buf, obuf, fs, fr, bs, br, own):
    gate_rows = bank_ref.shape[2]
    rows = 2 * gate_rows
    a = lax.axis_index("pb")
    w = lax.axis_index("wa")
    half = wa_count // 2
    w2 = w // half
    w0 = w % 2
    wm = w - w2 * half - w0

    peers = []
    for dw2 in (1, 0):
        for da in range(groups):
            for dw0 in range(2):
                if dw2 or da or dw0:
                    peers.append(((a + da) % groups, (w2 + dw2) % 2, (w0 + dw0) % 2))

    def device(p):
        return (p[0], p[1] * half + wm + p[2])

    def slot(p):
        return (p[2] * groups + p[0]) * 2 + p[1]

    def piece(ref, p, c):
        return ref.at[p[0] * 2 + p[1], :, p[2], c]

    def held(ref, c, s):
        return ref.at[c, pl.ds(s * mid, mid)]

    me = (a, w2, w0)
    mine = slot(me)

    def forward(c, p):
        return pltpu.make_async_remote_copy(
            src_ref=piece(x_ref, p, c), dst_ref=held(buf, c, mine),
            send_sem=fs.at[c, slot(p)], recv_sem=fr.at[c, mine],
            device_id=device(p), device_id_type=MESH)

    def arriving(c, p):
        return pltpu.make_async_remote_copy(
            src_ref=piece(x_ref, p, c), dst_ref=held(buf, c, slot(p)),
            send_sem=fs.at[c, slot(p)], recv_sem=fr.at[c, slot(p)],
            device_id=device(p), device_id_type=MESH)

    def back(c, p):
        return pltpu.make_async_remote_copy(
            src_ref=held(obuf, c, slot(p)), dst_ref=piece(out_ref, me, c),
            send_sem=bs.at[c, slot(p)], recv_sem=br.at[c, mine],
            device_id=device(p), device_id_type=MESH)

    def returning(c, p):
        return pltpu.make_async_remote_copy(
            src_ref=held(obuf, c, slot(p)), dst_ref=piece(out_ref, p, c),
            send_sem=bs.at[c, slot(p)], recv_sem=br.at[c, slot(p)],
            device_id=device(p), device_id_type=MESH)

    barrier = pltpu.get_barrier_semaphore()
    for p in peers:
        pl.semaphore_signal(barrier, inc=1, device_id=device(p), device_id_type=MESH)
    pl.semaphore_wait(barrier, len(peers))

    for c in range(CHUNKS):
        for p in peers:
            forward(c, p).start()
    stay = [pltpu.make_async_copy(piece(x_ref, me, c), held(buf, c, mine), own.at[0, c])
            for c in range(CHUNKS)]
    for copy in stay:
        copy.start()

    gates = [bank_ref[order_ref[k]] for k in range(4)]
    first = embed(gates[0][0], gates[0][1])
    third = embed(gates[2][0], gates[2][1])
    lanes_gate[...] = dot(third, first)
    real, imag = 0.0, 0.0
    for high in range(2):
        spread = spread_rows(groups, mid, gate_rows, high)
        real += dot_t(dot(spread, gates[3][0]), spread)
        imag += dot_t(dot(spread, gates[3][1]), spread)
    zero = jnp.zeros((gate_rows, gate_rows), jnp.float32)
    halves = []
    for part in range(2):
        g = gates[1][part]
        halves.append(jnp.concatenate([
            jnp.concatenate([g, zero], axis=1), jnp.concatenate([zero, g], axis=1)], axis=0))
    both = dot(embed(real, imag), jnp.concatenate(halves, axis=0))
    rows_gate[:, :rows] = both
    rows_gate[:rows, rows:] = -both[rows:]
    rows_gate[rows:, rows:] = both[:rows]

    for c in range(CHUNKS):
        for p in peers:
            arriving(c, p).wait_recv()
        stay[c].wait()
        flat_in = buf.at[c].reshape(rows * SUB, buf.shape[-1])
        flat_out = obuf.at[c].reshape(rows * SUB, buf.shape[-1])
        for q in range(SUB // 2):
            re = flat_in[pl.ds(2 * q, rows, SUB), :]
            im = flat_in[pl.ds(2 * q + 1, rows, SUB), :]
            mixed = dot_t(jnp.concatenate([re, im], axis=1), lanes_gate[...])
            tall = jnp.concatenate([mixed[:, :gate_rows], mixed[:, gate_rows:]], axis=0)
            done = dot(rows_gate[...], tall)
            flat_out[pl.ds(2 * q, rows, SUB), :] = done[:rows]
            flat_out[pl.ds(2 * q + 1, rows, SUB), :] = done[rows:]
        for p in peers:
            back(c, p).start()
        pltpu.make_async_copy(held(obuf, c, mine), piece(out_ref, me, c), own.at[1, c]).start()

    for c in range(CHUNKS):
        for p in peers:
            returning(c, p).wait_recv()
        pltpu.make_async_copy(held(obuf, c, mine), piece(out_ref, me, c), own.at[1, c]).wait()
    for c in range(CHUNKS):
        for p in peers:
            forward(c, p).wait_send()
            back(c, p).wait_send()


def per_device(groups, wa_count, state, gate_bank, pass_order):
    lanes = gate_bank.shape[2]
    mid = lanes // (2 * groups)
    size = state.shape[1]
    shape = (2 * groups, mid, 2, CHUNKS, SUB, lanes)
    x = state.reshape(2, size // lanes, lanes).transpose(1, 0, 2).reshape(shape)
    slots = 4 * groups
    out = pl.pallas_call(
        functools.partial(kernel, groups, wa_count, mid),
        out_shape=jax.ShapeDtypeStruct(shape, jnp.float32),
        in_specs=[
            pl.BlockSpec(memory_space=pltpu.SMEM),
            pl.BlockSpec(memory_space=pltpu.VMEM),
            pl.BlockSpec(memory_space=pl.ANY),
        ],
        out_specs=pl.BlockSpec(memory_space=pl.ANY),
        scratch_shapes=[
            pltpu.VMEM((2 * lanes, 2 * lanes), jnp.float32),
            pltpu.VMEM((4 * lanes, 4 * lanes), jnp.float32),
            pltpu.VMEM((CHUNKS, 2 * lanes, SUB, lanes), jnp.float32),
            pltpu.VMEM((CHUNKS, 2 * lanes, SUB, lanes), jnp.float32),
            pltpu.SemaphoreType.DMA((CHUNKS, slots)),
            pltpu.SemaphoreType.DMA((CHUNKS, slots)),
            pltpu.SemaphoreType.DMA((CHUNKS, slots)),
            pltpu.SemaphoreType.DMA((CHUNKS, slots)),
            pltpu.SemaphoreType.DMA((2, CHUNKS)),
        ],
        compiler_params=pltpu.CompilerParams(collective_id=0, has_side_effects=True),
    )(pass_order, gate_bank, x)
    return out.reshape(size // lanes, 2, lanes).transpose(1, 0, 2).reshape(2, size)


def solution(mesh):
    in_specs = (P(None, ("pb", "wa")), P(), P())
    out_specs = P(None, ("pb", "wa"))
    return jax.shard_map(
        functools.partial(per_device, mesh.shape["pb"], mesh.shape["wa"]),
        mesh=mesh, in_specs=in_specs, out_specs=out_specs, check_vma=False,
    )
```

```python
import functools

import jax
import jax.numpy as jnp
from jax import lax
from jax.experimental import pallas as pl
from jax.experimental.pallas import tpu as pltpu
from jax.sharding import PartitionSpec as P

MESH = pl.DeviceIdType.MESH
HIGH = lax.Precision.HIGHEST
CHUNKS = 2
SUB = 8


def dot(a, b):
    return lax.dot_general(
        a, b, (((1,), (0,)), ((), ())), precision=HIGH, preferred_element_type=jnp.float32
    )


def dot_t(a, b):
    return lax.dot_general(
        a, b, (((1,), (1,)), ((), ())), precision=HIGH, preferred_element_type=jnp.float32
    )


def embed(real, imag):
    upper = jnp.concatenate([real, -imag], axis=1)
    lower = jnp.concatenate([imag, real], axis=1)
    return jnp.concatenate([upper, lower], axis=0)


def spread_rows(groups, mid, gate_rows, high):
    slot = lax.broadcasted_iota(jnp.int32, (2 * gate_rows, gate_rows), 0)
    row = lax.broadcasted_iota(jnp.int32, (2 * gate_rows, gate_rows), 1)
    a = row // (2 * mid)
    w0 = (row // mid) % 2
    m = row % mid
    return jnp.where(slot == ((w0 * groups + a) * 2 + high) * mid + m, 1.0, 0.0).astype(jnp.float32)


def kernel(groups, wa_count, mid, order_ref, bank_ref, x_ref, out_ref, lanes_gate, rows_gate,
           buf, obuf, fs, fr, bs, br, own):
    gate_rows = bank_ref.shape[2]
    rows = 2 * gate_rows
    a = lax.axis_index("pb")
    w = lax.axis_index("wa")
    half = wa_count // 2
    w2 = w // half
    w0 = w % 2
    wm = w - w2 * half - w0

    peers = []
    for dw2 in (1, 0):
        for da in range(groups):
            for dw0 in range(2):
                if dw2 or da or dw0:
                    peers.append(((a + da) % groups, (w2 + dw2) % 2, (w0 + dw0) % 2))

    def device(p):
        return (p[0], p[1] * half + wm + p[2])

    def slot(p):
        return (p[2] * groups + p[0]) * 2 + p[1]

    def piece(ref, p, c):
        return ref.at[p[0] * 2 + p[1], :, p[2], c]

    def held(ref, c, s):
        return ref.at[c, pl.ds(s * mid, mid)]

    me = (a, w2, w0)
    mine = slot(me)

    def forward(c, p):
        return pltpu.make_async_remote_copy(
            src_ref=piece(x_ref, p, c), dst_ref=held(buf, c, mine),
            send_sem=fs.at[c, slot(p)], recv_sem=fr.at[c, mine],
            device_id=device(p), device_id_type=MESH)

    def arriving(c, p):
        return pltpu.make_async_remote_copy(
            src_ref=piece(x_ref, p, c), dst_ref=held(buf, c, slot(p)),
            send_sem=fs.at[c, slot(p)], recv_sem=fr.at[c, slot(p)],
            device_id=device(p), device_id_type=MESH)

    def back(c, p):
        return pltpu.make_async_remote_copy(
            src_ref=held(obuf, c, slot(p)), dst_ref=piece(out_ref, me, c),
            send_sem=bs.at[c, slot(p)], recv_sem=br.at[c, mine],
            device_id=device(p), device_id_type=MESH)

    def returning(c, p):
        return pltpu.make_async_remote_copy(
            src_ref=held(obuf, c, slot(p)), dst_ref=piece(out_ref, p, c),
            send_sem=bs.at[c, slot(p)], recv_sem=br.at[c, slot(p)],
            device_id=device(p), device_id_type=MESH)

    barrier = pltpu.get_barrier_semaphore()
    for p in peers:
        pl.semaphore_signal(barrier, inc=1, device_id=device(p), device_id_type=MESH)
    pl.semaphore_wait(barrier, len(peers))

    for c in range(CHUNKS):
        for p in peers:
            forward(c, p).start()
    stay = [pltpu.make_async_copy(piece(x_ref, me, c), held(buf, c, mine), own.at[0, c])
            for c in range(CHUNKS)]
    for copy in stay:
        copy.start()

    gates = [bank_ref[order_ref[k]] for k in range(4)]
    first = embed(gates[0][0], gates[0][1])
    third = embed(gates[2][0], gates[2][1])
    lanes_gate[...] = dot(third, first)
    real, imag = 0.0, 0.0
    for high in range(2):
        spread = spread_rows(groups, mid, gate_rows, high)
        real += dot_t(dot(spread, gates[3][0]), spread)
        imag += dot_t(dot(spread, gates[3][1]), spread)
    zero = jnp.zeros((gate_rows, gate_rows), jnp.float32)
    halves = []
    for part in range(2):
        g = gates[1][part]
        halves.append(jnp.concatenate([
            jnp.concatenate([g, zero], axis=1), jnp.concatenate([zero, g], axis=1)], axis=0))
    both = dot(embed(real, imag), jnp.concatenate(halves, axis=0))
    rows_gate[:, :rows] = both
    rows_gate[:rows, rows:] = -both[rows:]
    rows_gate[rows:, rows:] = both[:rows]

    for c in range(CHUNKS):
        for p in peers:
            arriving(c, p).wait_recv()
        stay[c].wait()
        flat_in = buf.at[c].reshape(rows * SUB, buf.shape[-1])
        flat_out = obuf.at[c].reshape(rows * SUB, buf.shape[-1])
        for q in range(SUB // 2):
            re = flat_in[pl.ds(2 * q, rows, SUB), :]
            im = flat_in[pl.ds(2 * q + 1, rows, SUB), :]
            mixed = dot_t(jnp.concatenate([re, im], axis=1), lanes_gate[...])
            tall = jnp.concatenate([mixed[:, :gate_rows], mixed[:, gate_rows:]], axis=0)
            done = dot(rows_gate[...], tall)
            flat_out[pl.ds(2 * q, rows, SUB), :] = done[:rows]
            flat_out[pl.ds(2 * q + 1, rows, SUB), :] = done[rows:]
        for p in peers:
            back(c, p).start()
        pltpu.make_async_copy(held(obuf, c, mine), piece(out_ref, me, c), own.at[1, c]).start()

    for c in range(CHUNKS):
        for p in peers:
            returning(c, p).wait_recv()
        pltpu.make_async_copy(held(obuf, c, mine), piece(out_ref, me, c), own.at[1, c]).wait()
    for c in range(CHUNKS):
        for p in peers:
            forward(c, p).wait_send()
            back(c, p).wait_send()


def per_device(groups, wa_count, state, gate_bank, pass_order):
    lanes = gate_bank.shape[2]
    mid = lanes // (2 * groups)
    size = state.shape[1]
    shape = (2 * groups, mid, 2, CHUNKS, SUB, lanes)
    x = state.reshape(2, size // lanes, lanes).transpose(1, 0, 2).reshape(shape)
    slots = 4 * groups
    out = pl.pallas_call(
        functools.partial(kernel, groups, wa_count, mid),
        out_shape=pltpu.VMEM(shape, jnp.float32),
        in_specs=[
            pl.BlockSpec(memory_space=pltpu.SMEM),
            pl.BlockSpec(memory_space=pltpu.VMEM),
            pl.BlockSpec(memory_space=pl.ANY),
        ],
        out_specs=pl.BlockSpec(memory_space=pltpu.VMEM),
        scratch_shapes=[
            pltpu.VMEM((2 * lanes, 2 * lanes), jnp.float32),
            pltpu.VMEM((4 * lanes, 4 * lanes), jnp.float32),
            pltpu.VMEM((CHUNKS, 2 * lanes, SUB, lanes), jnp.float32),
            pltpu.VMEM((CHUNKS, 2 * lanes, SUB, lanes), jnp.float32),
            pltpu.SemaphoreType.DMA((CHUNKS, slots)),
            pltpu.SemaphoreType.DMA((CHUNKS, slots)),
            pltpu.SemaphoreType.DMA((CHUNKS, slots)),
            pltpu.SemaphoreType.DMA((CHUNKS, slots)),
            pltpu.SemaphoreType.DMA((2, CHUNKS)),
        ],
        compiler_params=pltpu.CompilerParams(collective_id=0, has_side_effects=True),
    )(pass_order, gate_bank, x)
    return out.reshape(size // lanes, 2, lanes).transpose(1, 0, 2).reshape(2, size)


def solution(mesh):
    in_specs = (P(None, ("pb", "wa")), P(), P())
    out_specs = P(None, ("pb", "wa"))
    return jax.shard_map(
        functools.partial(per_device, mesh.shape["pb"], mesh.shape["wa"]),
        mesh=mesh, in_specs=in_specs, out_specs=out_specs, check_vma=False,
    )
```

```python
import functools

import jax
import jax.numpy as jnp
from jax import lax
from jax.experimental import pallas as pl
from jax.experimental.pallas import tpu as pltpu
from jax.sharding import PartitionSpec as P

MESH = pl.DeviceIdType.MESH
HIGH = lax.Precision.HIGHEST
CHUNKS = 2
SUB = 8


def dot(a, b):
    return lax.dot_general(
        a, b, (((1,), (0,)), ((), ())), precision=HIGH, preferred_element_type=jnp.float32
    )


def dot_t(a, b):
    return lax.dot_general(
        a, b, (((1,), (1,)), ((), ())), precision=HIGH, preferred_element_type=jnp.float32
    )


def embed(real, imag):
    upper = jnp.concatenate([real, -imag], axis=1)
    lower = jnp.concatenate([imag, real], axis=1)
    return jnp.concatenate([upper, lower], axis=0)


def spread_rows(groups, mid, gate_rows, high):
    slot = lax.broadcasted_iota(jnp.int32, (2 * gate_rows, gate_rows), 0)
    row = lax.broadcasted_iota(jnp.int32, (2 * gate_rows, gate_rows), 1)
    a = row // (2 * mid)
    w0 = (row // mid) % 2
    m = row % mid
    return jnp.where(slot == ((w0 * groups + a) * 2 + high) * mid + m, 1.0, 0.0).astype(jnp.float32)


def kernel(groups, wa_count, mid, order_hbm, bank_hbm, x_ref, out_ref, order_ref, bank_ref,
           lanes_gate, rows_gate, buf, obuf, fs, fr, bs, br, own, load, round_sem):
    gate_rows = bank_ref.shape[2]
    rows = 2 * gate_rows
    a = lax.axis_index("pb")
    w = lax.axis_index("wa")
    half = wa_count // 2
    w2 = w // half
    w0 = w % 2
    wm = w - w2 * half - w0

    peers = []
    for dw2 in (1, 0):
        for da in range(groups):
            for dw0 in range(2):
                if dw2 or da or dw0:
                    peers.append(((a + da) % groups, (w2 + dw2) % 2, (w0 + dw0) % 2))

    def device(p):
        return (p[0], p[1] * half + wm + p[2])

    def slot(p):
        return (p[2] * groups + p[0]) * 2 + p[1]

    def piece(ref, p, c):
        return ref.at[p[0] * 2 + p[1], :, p[2], c]

    def held(ref, c, s):
        return ref.at[c, pl.ds(s * mid, mid)]

    me = (a, w2, w0)
    mine = slot(me)

    def forward(c, p):
        return pltpu.make_async_remote_copy(
            src_ref=piece(x_ref, p, c), dst_ref=held(buf, c, mine),
            send_sem=fs.at[c, slot(p)], recv_sem=fr.at[c, mine],
            device_id=device(p), device_id_type=MESH)

    def arriving(c, p):
        return pltpu.make_async_remote_copy(
            src_ref=piece(x_ref, p, c), dst_ref=held(buf, c, slot(p)),
            send_sem=fs.at[c, slot(p)], recv_sem=fr.at[c, slot(p)],
            device_id=device(p), device_id_type=MESH)

    def back(c, p):
        return pltpu.make_async_remote_copy(
            src_ref=held(obuf, c, slot(p)), dst_ref=piece(out_ref, me, c),
            send_sem=bs.at[c, slot(p)], recv_sem=br.at[c, mine],
            device_id=device(p), device_id_type=MESH)

    def returning(c, p):
        return pltpu.make_async_remote_copy(
            src_ref=held(obuf, c, slot(p)), dst_ref=piece(out_ref, p, c),
            send_sem=bs.at[c, slot(p)], recv_sem=br.at[c, slot(p)],
            device_id=device(p), device_id_type=MESH)

    across = (a, (w2 + 1) % 2, w0)
    steps = [(a, w2, (w0 + 1) % 2)]
    stride = 1
    while stride < groups:
        steps.append((a + stride * (1 - 2 * ((a // stride) % 2)), w2, w0))
        stride *= 2

    barrier = pltpu.get_barrier_semaphore()
    for p in [across] + steps:
        pl.semaphore_signal(barrier, inc=1, device_id=device(p), device_id_type=MESH)
    pl.semaphore_wait(barrier, 1 + len(steps))

    forward(0, across).start()
    for k, p in enumerate(steps):
        pl.semaphore_signal(round_sem.at[k], inc=1, device_id=device(p), device_id_type=MESH)
        pl.semaphore_wait(round_sem.at[k], 1)

    for c in range(CHUNKS):
        for p in peers[1 if c == 0 else 0:]:
            forward(c, p).start()
    fetch = [pltpu.make_async_copy(order_hbm, order_ref, load.at[0]),
             pltpu.make_async_copy(bank_hbm, bank_ref, load.at[1])]
    stay = [pltpu.make_async_copy(piece(x_ref, me, c), held(buf, c, mine), own.at[0, c])
            for c in range(CHUNKS)]
    for copy in fetch + stay:
        copy.start()
    for copy in fetch:
        copy.wait()

    gates = [bank_ref[order_ref[k]] for k in range(4)]
    first = embed(gates[0][0], gates[0][1])
    third = embed(gates[2][0], gates[2][1])
    lanes_gate[...] = dot(third, first)
    real, imag = 0.0, 0.0
    for high in range(2):
        spread = spread_rows(groups, mid, gate_rows, high)
        real += dot_t(dot(spread, gates[3][0]), spread)
        imag += dot_t(dot(spread, gates[3][1]), spread)
    zero = jnp.zeros((gate_rows, gate_rows), jnp.float32)
    halves = []
    for part in range(2):
        g = gates[1][part]
        halves.append(jnp.concatenate([
            jnp.concatenate([g, zero], axis=1), jnp.concatenate([zero, g], axis=1)], axis=0))
    both = dot(embed(real, imag), jnp.concatenate(halves, axis=0))
    rows_gate[:, :rows] = both
    rows_gate[:rows, rows:] = -both[rows:]
    rows_gate[rows:, rows:] = both[:rows]

    for c in range(CHUNKS):
        for p in peers:
            arriving(c, p).wait_recv()
        stay[c].wait()
        flat_in = buf.at[c].reshape(rows * SUB, buf.shape[-1])
        flat_out = obuf.at[c].reshape(rows * SUB, buf.shape[-1])
        for q in range(SUB // 2):
            re = flat_in[pl.ds(2 * q, rows, SUB), :]
            im = flat_in[pl.ds(2 * q + 1, rows, SUB), :]
            mixed = dot_t(jnp.concatenate([re, im], axis=1), lanes_gate[...])
            tall = jnp.concatenate([mixed[:, :gate_rows], mixed[:, gate_rows:]], axis=0)
            done = dot(rows_gate[...], tall)
            flat_out[pl.ds(2 * q, rows, SUB), :] = done[:rows]
            flat_out[pl.ds(2 * q + 1, rows, SUB), :] = done[rows:]
        for p in peers:
            back(c, p).start()
        pltpu.make_async_copy(held(obuf, c, mine), piece(out_ref, me, c), own.at[1, c]).start()

    for c in range(CHUNKS):
        for p in peers:
            returning(c, p).wait_recv()
        pltpu.make_async_copy(held(obuf, c, mine), piece(out_ref, me, c), own.at[1, c]).wait()
    for c in range(CHUNKS):
        for p in peers:
            forward(c, p).wait_send()
            back(c, p).wait_send()


def per_device(groups, wa_count, state, gate_bank, pass_order):
    lanes = gate_bank.shape[2]
    mid = lanes // (2 * groups)
    size = state.shape[1]
    shape = (2 * groups, mid, 2, CHUNKS, SUB, lanes)
    x = state.reshape(2, size // lanes, lanes).transpose(1, 0, 2).reshape(shape)
    slots = 4 * groups
    out = pl.pallas_call(
        functools.partial(kernel, groups, wa_count, mid),
        out_shape=pltpu.VMEM(shape, jnp.float32),
        in_specs=[
            pl.BlockSpec(memory_space=pl.ANY),
            pl.BlockSpec(memory_space=pl.ANY),
            pl.BlockSpec(memory_space=pl.ANY),
        ],
        out_specs=pl.BlockSpec(memory_space=pltpu.VMEM),
        scratch_shapes=[
            pltpu.SMEM(pass_order.shape, jnp.int32),
            pltpu.VMEM(gate_bank.shape, jnp.float32),
            pltpu.VMEM((2 * lanes, 2 * lanes), jnp.float32),
            pltpu.VMEM((4 * lanes, 4 * lanes), jnp.float32),
            pltpu.VMEM((CHUNKS, 2 * lanes, SUB, lanes), jnp.float32),
            pltpu.VMEM((CHUNKS, 2 * lanes, SUB, lanes), jnp.float32),
            pltpu.SemaphoreType.DMA((CHUNKS, slots)),
            pltpu.SemaphoreType.DMA((CHUNKS, slots)),
            pltpu.SemaphoreType.DMA((CHUNKS, slots)),
            pltpu.SemaphoreType.DMA((CHUNKS, slots)),
            pltpu.SemaphoreType.DMA((2, CHUNKS)),
            pltpu.SemaphoreType.DMA((2,)),
            pltpu.SemaphoreType.REGULAR((groups.bit_length(),)),
        ],
        compiler_params=pltpu.CompilerParams(collective_id=0, has_side_effects=True),
    )(pass_order, gate_bank, x)
    return out.reshape(size // lanes, 2, lanes).transpose(1, 0, 2).reshape(2, size)


def solution(mesh):
    in_specs = (P(None, ("pb", "wa")), P(), P())
    out_specs = P(None, ("pb", "wa"))
    return jax.shard_map(
        functools.partial(per_device, mesh.shape["pb"], mesh.shape["wa"]),
        mesh=mesh, in_specs=in_specs, out_specs=out_specs, check_vma=False,
    )
```

```python
import functools

import jax
import jax.numpy as jnp
from jax import lax
from jax.experimental import pallas as pl
from jax.experimental.pallas import tpu as pltpu
from jax.sharding import PartitionSpec as P

MESH = pl.DeviceIdType.MESH
HIGH = lax.Precision.HIGHEST
CHUNKS = 2
SUB = 8


def dot(a, b):
    return lax.dot_general(
        a, b, (((1,), (0,)), ((), ())), precision=HIGH, preferred_element_type=jnp.float32
    )


def dot_t(a, b):
    return lax.dot_general(
        a, b, (((1,), (1,)), ((), ())), precision=HIGH, preferred_element_type=jnp.float32
    )


def embed(real, imag):
    upper = jnp.concatenate([real, -imag], axis=1)
    lower = jnp.concatenate([imag, real], axis=1)
    return jnp.concatenate([upper, lower], axis=0)


def spread_rows(groups, mid, gate_rows, high):
    slot = lax.broadcasted_iota(jnp.int32, (2 * gate_rows, gate_rows), 0)
    row = lax.broadcasted_iota(jnp.int32, (2 * gate_rows, gate_rows), 1)
    a = row // (2 * mid)
    w0 = (row // mid) % 2
    m = row % mid
    return jnp.where(slot == ((w0 * groups + a) * 2 + high) * mid + m, 1.0, 0.0).astype(jnp.float32)


def kernel(groups, wa_count, mid, order_hbm, bank_hbm, x_ref, out_ref, order_ref, bank_ref,
           lanes_gate, rows_gate, buf, obuf, fs, fr, bs, br, own, load, round_sem):
    gate_rows = bank_ref.shape[2]
    rows = 2 * gate_rows
    a = lax.axis_index("pb")
    w = lax.axis_index("wa")
    half = wa_count // 2
    w2 = w // half
    w0 = w % 2
    wm = w - w2 * half - w0

    peers = []
    for dw2 in (1, 0):
        for da in range(groups):
            for dw0 in range(2):
                if dw2 or da or dw0:
                    peers.append(((a + da) % groups, (w2 + dw2) % 2, (w0 + dw0) % 2))

    def device(p):
        return (p[0], p[1] * half + wm + p[2])

    def slot(p):
        return (p[2] * groups + p[0]) * 2 + p[1]

    def piece(ref, p, c):
        return ref.at[p[0] * 2 + p[1], :, p[2], c]

    def held(ref, c, s):
        return ref.at[c, pl.ds(s * mid, mid)]

    me = (a, w2, w0)
    mine = slot(me)

    def forward(c, p):
        return pltpu.make_async_remote_copy(
            src_ref=piece(x_ref, p, c), dst_ref=held(buf, c, mine),
            send_sem=fs.at[c, slot(p)], recv_sem=fr.at[c, mine],
            device_id=device(p), device_id_type=MESH)

    def arriving(c, p):
        return pltpu.make_async_remote_copy(
            src_ref=piece(x_ref, p, c), dst_ref=held(buf, c, slot(p)),
            send_sem=fs.at[c, slot(p)], recv_sem=fr.at[c, slot(p)],
            device_id=device(p), device_id_type=MESH)

    def back(c, p):
        return pltpu.make_async_remote_copy(
            src_ref=held(obuf, c, slot(p)), dst_ref=piece(out_ref, me, c),
            send_sem=bs.at[c, slot(p)], recv_sem=br.at[c, mine],
            device_id=device(p), device_id_type=MESH)

    def returning(c, p):
        return pltpu.make_async_remote_copy(
            src_ref=held(obuf, c, slot(p)), dst_ref=piece(out_ref, p, c),
            send_sem=bs.at[c, slot(p)], recv_sem=br.at[c, slot(p)],
            device_id=device(p), device_id_type=MESH)

    across = (a, (w2 + 1) % 2, w0)
    steps = [(a, w2, (w0 + 1) % 2)]
    stride = 1
    while stride < groups:
        steps.append((a + stride * (1 - 2 * ((a // stride) % 2)), w2, w0))
        stride *= 2

    barrier = pltpu.get_barrier_semaphore()
    for p in [across] + steps:
        pl.semaphore_signal(barrier, inc=1, device_id=device(p), device_id_type=MESH)
    pl.semaphore_wait(barrier, 1 + len(steps))

    ends = w2 == 2 * wm // half
    far = peers[:2 * groups]
    near = peers[2 * groups:]
    marker = near[1]

    @pl.when(jnp.logical_not(ends))
    def _():
        forward(0, across).start()

    for k, p in enumerate(steps):
        pl.semaphore_signal(round_sem.at[k], inc=1, device_id=device(p), device_id_type=MESH)
        pl.semaphore_wait(round_sem.at[k], 1)

    for p in near:
        forward(0, p).start()

    @pl.when(ends)
    def _():
        forward(0, marker).wait_send()
        forward(0, across).start()

    for p in far[1:]:
        forward(0, p).start()
    for c in range(1, CHUNKS):
        for p in peers:
            forward(c, p).start()
    fetch = [pltpu.make_async_copy(order_hbm, order_ref, load.at[0]),
             pltpu.make_async_copy(bank_hbm, bank_ref, load.at[1])]
    stay = [pltpu.make_async_copy(piece(x_ref, me, c), held(buf, c, mine), own.at[0, c])
            for c in range(CHUNKS)]
    for copy in fetch + stay:
        copy.start()
    for copy in fetch:
        copy.wait()

    gates = [bank_ref[order_ref[k]] for k in range(4)]
    first = embed(gates[0][0], gates[0][1])
    third = embed(gates[2][0], gates[2][1])
    lanes_gate[...] = dot(third, first)
    real, imag = 0.0, 0.0
    for high in range(2):
        spread = spread_rows(groups, mid, gate_rows, high)
        real += dot_t(dot(spread, gates[3][0]), spread)
        imag += dot_t(dot(spread, gates[3][1]), spread)
    zero = jnp.zeros((gate_rows, gate_rows), jnp.float32)
    halves = []
    for part in range(2):
        g = gates[1][part]
        halves.append(jnp.concatenate([
            jnp.concatenate([g, zero], axis=1), jnp.concatenate([zero, g], axis=1)], axis=0))
    both = dot(embed(real, imag), jnp.concatenate(halves, axis=0))
    rows_gate[:, :rows] = both
    rows_gate[:rows, rows:] = -both[rows:]
    rows_gate[rows:, rows:] = both[:rows]

    for c in range(CHUNKS):
        for p in peers:
            arriving(c, p).wait_recv()
        stay[c].wait()
        flat_in = buf.at[c].reshape(rows * SUB, buf.shape[-1])
        flat_out = obuf.at[c].reshape(rows * SUB, buf.shape[-1])
        for q in range(SUB // 2):
            re = flat_in[pl.ds(2 * q, rows, SUB), :]
            im = flat_in[pl.ds(2 * q + 1, rows, SUB), :]
            mixed = dot_t(jnp.concatenate([re, im], axis=1), lanes_gate[...])
            tall = jnp.concatenate([mixed[:, :gate_rows], mixed[:, gate_rows:]], axis=0)
            done = dot(rows_gate[...], tall)
            flat_out[pl.ds(2 * q, rows, SUB), :] = done[:rows]
            flat_out[pl.ds(2 * q + 1, rows, SUB), :] = done[rows:]
        for p in peers:
            back(c, p).start()
        pltpu.make_async_copy(held(obuf, c, mine), piece(out_ref, me, c), own.at[1, c]).start()

    for c in range(CHUNKS):
        for p in peers:
            returning(c, p).wait_recv()
        pltpu.make_async_copy(held(obuf, c, mine), piece(out_ref, me, c), own.at[1, c]).wait()
    for c in range(CHUNKS):
        for p in peers:
            if c or p is not marker:
                forward(c, p).wait_send()
            back(c, p).wait_send()

    @pl.when(jnp.logical_not(ends))
    def _():
        forward(0, marker).wait_send()


def per_device(groups, wa_count, state, gate_bank, pass_order):
    lanes = gate_bank.shape[2]
    mid = lanes // (2 * groups)
    size = state.shape[1]
    shape = (2 * groups, mid, 2, CHUNKS, SUB, lanes)
    x = state.reshape(2, size // lanes, lanes).transpose(1, 0, 2).reshape(shape)
    slots = 4 * groups
    out = pl.pallas_call(
        functools.partial(kernel, groups, wa_count, mid),
        out_shape=pltpu.VMEM(shape, jnp.float32),
        in_specs=[
            pl.BlockSpec(memory_space=pl.ANY),
            pl.BlockSpec(memory_space=pl.ANY),
            pl.BlockSpec(memory_space=pl.ANY),
        ],
        out_specs=pl.BlockSpec(memory_space=pltpu.VMEM),
        scratch_shapes=[
            pltpu.SMEM(pass_order.shape, jnp.int32),
            pltpu.VMEM(gate_bank.shape, jnp.float32),
            pltpu.VMEM((2 * lanes, 2 * lanes), jnp.float32),
            pltpu.VMEM((4 * lanes, 4 * lanes), jnp.float32),
            pltpu.VMEM((CHUNKS, 2 * lanes, SUB, lanes), jnp.float32),
            pltpu.VMEM((CHUNKS, 2 * lanes, SUB, lanes), jnp.float32),
            pltpu.SemaphoreType.DMA((CHUNKS, slots)),
            pltpu.SemaphoreType.DMA((CHUNKS, slots)),
            pltpu.SemaphoreType.DMA((CHUNKS, slots)),
            pltpu.SemaphoreType.DMA((CHUNKS, slots)),
            pltpu.SemaphoreType.DMA((2, CHUNKS)),
            pltpu.SemaphoreType.DMA((2,)),
            pltpu.SemaphoreType.REGULAR((groups.bit_length(),)),
        ],
        compiler_params=pltpu.CompilerParams(collective_id=0, has_side_effects=True),
    )(pass_order, gate_bank, x)
    return out.reshape(size // lanes, 2, lanes).transpose(1, 0, 2).reshape(2, size)


def solution(mesh):
    in_specs = (P(None, ("pb", "wa")), P(), P())
    out_specs = P(None, ("pb", "wa"))
    return jax.shard_map(
        functools.partial(per_device, mesh.shape["pb"], mesh.shape["wa"]),
        mesh=mesh, in_specs=in_specs, out_specs=out_specs, check_vma=False,
    )
```

```python
import functools

import jax
import jax.numpy as jnp
from jax import lax
from jax.experimental import pallas as pl
from jax.experimental.pallas import tpu as pltpu
from jax.sharding import PartitionSpec as P

MESH = pl.DeviceIdType.MESH
HIGH = lax.Precision.HIGHEST
CHUNKS = 2
SUB = 8


def dot(a, b):
    return lax.dot_general(
        a, b, (((1,), (0,)), ((), ())), precision=HIGH, preferred_element_type=jnp.float32
    )


def dot_t(a, b):
    return lax.dot_general(
        a, b, (((1,), (1,)), ((), ())), precision=HIGH, preferred_element_type=jnp.float32
    )


def embed(real, imag):
    upper = jnp.concatenate([real, -imag], axis=1)
    lower = jnp.concatenate([imag, real], axis=1)
    return jnp.concatenate([upper, lower], axis=0)


def spread_rows(groups, mid, gate_rows, high):
    slot = lax.broadcasted_iota(jnp.int32, (2 * gate_rows, gate_rows), 0)
    row = lax.broadcasted_iota(jnp.int32, (2 * gate_rows, gate_rows), 1)
    a = row // (2 * mid)
    w0 = (row // mid) % 2
    m = row % mid
    return jnp.where(slot == ((w0 * groups + a) * 2 + high) * mid + m, 1.0, 0.0).astype(jnp.float32)


def kernel(groups, wa_count, mid, order_hbm, bank_hbm, x_ref, out_ref, order_ref, bank_ref,
           lanes_gate, rows_gate, buf, obuf, fs, fr, bs, br, own, load, round_sem):
    gate_rows = bank_ref.shape[2]
    rows = 2 * gate_rows
    a = lax.axis_index("pb")
    w = lax.axis_index("wa")
    half = wa_count // 2
    w2 = w // half
    w0 = w % 2
    wm = w - w2 * half - w0

    peers = []
    for dw2 in (1, 0):
        for da in range(groups):
            for dw0 in range(2):
                if dw2 or da or dw0:
                    peers.append(((a + da) % groups, (w2 + dw2) % 2, (w0 + dw0) % 2))

    def device(p):
        return (p[0], p[1] * half + wm + p[2])

    def slot(p):
        return (p[2] * groups + p[0]) * 2 + p[1]

    def piece(ref, p, c):
        return ref.at[p[0] * 2 + p[1], :, p[2], c]

    def held(ref, c, s):
        return ref.at[c, pl.ds(s * mid, mid)]

    me = (a, w2, w0)
    mine = slot(me)

    def forward(c, p):
        return pltpu.make_async_remote_copy(
            src_ref=piece(x_ref, p, c), dst_ref=held(buf, c, mine),
            send_sem=fs.at[c, slot(p)], recv_sem=fr.at[c, mine],
            device_id=device(p), device_id_type=MESH)

    def arriving(c, p):
        return pltpu.make_async_remote_copy(
            src_ref=piece(x_ref, p, c), dst_ref=held(buf, c, slot(p)),
            send_sem=fs.at[c, slot(p)], recv_sem=fr.at[c, slot(p)],
            device_id=device(p), device_id_type=MESH)

    def back(c, p):
        return pltpu.make_async_remote_copy(
            src_ref=held(obuf, c, slot(p)), dst_ref=piece(out_ref, me, c),
            send_sem=bs.at[c, slot(p)], recv_sem=br.at[c, mine],
            device_id=device(p), device_id_type=MESH)

    def returning(c, p):
        return pltpu.make_async_remote_copy(
            src_ref=held(obuf, c, slot(p)), dst_ref=piece(out_ref, p, c),
            send_sem=bs.at[c, slot(p)], recv_sem=br.at[c, slot(p)],
            device_id=device(p), device_id_type=MESH)

    across = (a, (w2 + 1) % 2, w0)
    steps = [(a, w2, (w0 + 1) % 2)]
    stride = 1
    while stride < groups:
        steps.append((a + stride * (1 - 2 * ((a // stride) % 2)), w2, w0))
        stride *= 2

    ends = w2 == 2 * wm // half
    far = peers[:2 * groups]

    barrier = pltpu.get_barrier_semaphore()
    for p in [across] + steps:
        pl.semaphore_signal(barrier, inc=1, device_id=device(p), device_id_type=MESH)
    pl.semaphore_wait(barrier, 1 + len(steps))

    forward(0, across).start()
    for k, p in enumerate(steps):
        pl.semaphore_signal(round_sem.at[k], inc=1, device_id=device(p), device_id_type=MESH)
        pl.semaphore_wait(round_sem.at[k], 1)

    for c in range(CHUNKS):
        for p in peers[1 if c == 0 else 0:]:
            forward(c, p).start()
    fetch = [pltpu.make_async_copy(order_hbm, order_ref, load.at[0]),
             pltpu.make_async_copy(bank_hbm, bank_ref, load.at[1])]
    stay = [pltpu.make_async_copy(piece(x_ref, me, c), held(buf, c, mine), own.at[0, c])
            for c in range(CHUNKS)]
    for copy in fetch + stay:
        copy.start()
    for copy in fetch:
        copy.wait()

    gates = [bank_ref[order_ref[k]] for k in range(4)]
    first = embed(gates[0][0], gates[0][1])
    third = embed(gates[2][0], gates[2][1])
    lanes_gate[...] = dot(third, first)
    real, imag = 0.0, 0.0
    for high in range(2):
        spread = spread_rows(groups, mid, gate_rows, high)
        real += dot_t(dot(spread, gates[3][0]), spread)
        imag += dot_t(dot(spread, gates[3][1]), spread)
    zero = jnp.zeros((gate_rows, gate_rows), jnp.float32)
    halves = []
    for part in range(2):
        g = gates[1][part]
        halves.append(jnp.concatenate([
            jnp.concatenate([g, zero], axis=1), jnp.concatenate([zero, g], axis=1)], axis=0))
    both = dot(embed(real, imag), jnp.concatenate(halves, axis=0))
    rows_gate[:, :rows] = both
    rows_gate[:rows, rows:] = -both[rows:]
    rows_gate[rows:, rows:] = both[:rows]

    for c in range(CHUNKS):
        for p in peers:
            arriving(c, p).wait_recv()
        stay[c].wait()
        flat_in = buf.at[c].reshape(rows * SUB, buf.shape[-1])
        flat_out = obuf.at[c].reshape(rows * SUB, buf.shape[-1])
        for q in range(SUB // 2):
            re = flat_in[pl.ds(2 * q, rows, SUB), :]
            im = flat_in[pl.ds(2 * q + 1, rows, SUB), :]
            mixed = dot_t(jnp.concatenate([re, im], axis=1), lanes_gate[...])
            tall = jnp.concatenate([mixed[:, :gate_rows], mixed[:, gate_rows:]], axis=0)
            done = dot(rows_gate[...], tall)
            flat_out[pl.ds(2 * q, rows, SUB), :] = done[:rows]
            flat_out[pl.ds(2 * q + 1, rows, SUB), :] = done[rows:]
        if c:
            @pl.when(ends)
            def _():
                for p in far:
                    back(c - 1, p).wait_send()

        for p in peers:
            back(c, p).start()
        pltpu.make_async_copy(held(obuf, c, mine), piece(out_ref, me, c), own.at[1, c]).start()

    for c in range(CHUNKS):
        for p in peers:
            returning(c, p).wait_recv()
        pltpu.make_async_copy(held(obuf, c, mine), piece(out_ref, me, c), own.at[1, c]).wait()
    for c in range(CHUNKS):
        for p in peers:
            forward(c, p).wait_send()
        for p in peers[2 * groups if c + 1 < CHUNKS else 0:]:
            back(c, p).wait_send()

    @pl.when(jnp.logical_not(ends))
    def _():
        for c in range(CHUNKS - 1):
            for p in far:
                back(c, p).wait_send()


def per_device(groups, wa_count, state, gate_bank, pass_order):
    lanes = gate_bank.shape[2]
    mid = lanes // (2 * groups)
    size = state.shape[1]
    shape = (2 * groups, mid, 2, CHUNKS, SUB, lanes)
    x = state.reshape(2, size // lanes, lanes).transpose(1, 0, 2).reshape(shape)
    slots = 4 * groups
    out = pl.pallas_call(
        functools.partial(kernel, groups, wa_count, mid),
        out_shape=pltpu.VMEM(shape, jnp.float32),
        in_specs=[
            pl.BlockSpec(memory_space=pl.ANY),
            pl.BlockSpec(memory_space=pl.ANY),
            pl.BlockSpec(memory_space=pl.ANY),
        ],
        out_specs=pl.BlockSpec(memory_space=pltpu.VMEM),
        scratch_shapes=[
            pltpu.SMEM(pass_order.shape, jnp.int32),
            pltpu.VMEM(gate_bank.shape, jnp.float32),
            pltpu.VMEM((2 * lanes, 2 * lanes), jnp.float32),
            pltpu.VMEM((4 * lanes, 4 * lanes), jnp.float32),
            pltpu.VMEM((CHUNKS, 2 * lanes, SUB, lanes), jnp.float32),
            pltpu.VMEM((CHUNKS, 2 * lanes, SUB, lanes), jnp.float32),
            pltpu.SemaphoreType.DMA((CHUNKS, slots)),
            pltpu.SemaphoreType.DMA((CHUNKS, slots)),
            pltpu.SemaphoreType.DMA((CHUNKS, slots)),
            pltpu.SemaphoreType.DMA((CHUNKS, slots)),
            pltpu.SemaphoreType.DMA((2, CHUNKS)),
            pltpu.SemaphoreType.DMA((2,)),
            pltpu.SemaphoreType.REGULAR((groups.bit_length(),)),
        ],
        compiler_params=pltpu.CompilerParams(collective_id=0, has_side_effects=True),
    )(pass_order, gate_bank, x)
    return out.reshape(size // lanes, 2, lanes).transpose(1, 0, 2).reshape(2, size)


def solution(mesh):
    in_specs = (P(None, ("pb", "wa")), P(), P())
    out_specs = P(None, ("pb", "wa"))
    return jax.shard_map(
        functools.partial(per_device, mesh.shape["pb"], mesh.shape["wa"]),
        mesh=mesh, in_specs=in_specs, out_specs=out_specs, check_vma=False,
    )
```

```python
import functools

import jax
import jax.numpy as jnp
from jax import lax
from jax.experimental import pallas as pl
from jax.experimental.pallas import tpu as pltpu
from jax.sharding import PartitionSpec as P

MESH = pl.DeviceIdType.MESH
HIGH = lax.Precision.HIGHEST
CHUNKS = 2
SUB = 8


def dot(a, b):
    return lax.dot_general(
        a, b, (((1,), (0,)), ((), ())), precision=HIGH, preferred_element_type=jnp.float32
    )


def dot_t(a, b):
    return lax.dot_general(
        a, b, (((1,), (1,)), ((), ())), precision=HIGH, preferred_element_type=jnp.float32
    )


def embed(real, imag):
    upper = jnp.concatenate([real, -imag], axis=1)
    lower = jnp.concatenate([imag, real], axis=1)
    return jnp.concatenate([upper, lower], axis=0)


def spread_rows(groups, mid, gate_rows, high):
    slot = lax.broadcasted_iota(jnp.int32, (2 * gate_rows, gate_rows), 0)
    row = lax.broadcasted_iota(jnp.int32, (2 * gate_rows, gate_rows), 1)
    a = row // (2 * mid)
    w0 = (row // mid) % 2
    m = row % mid
    return jnp.where(slot == ((w0 * groups + a) * 2 + high) * mid + m, 1.0, 0.0).astype(jnp.float32)


def kernel(groups, wa_count, mid, order_hbm, bank_hbm, x_ref, out_ref, order_ref, bank_ref,
           lanes_gate, rows_gate, buf, obuf, fs, fr, bs, br, own, load, round_sem):
    gate_rows = bank_ref.shape[2]
    rows = 2 * gate_rows
    a = lax.axis_index("pb")
    w = lax.axis_index("wa")
    half = wa_count // 2
    w2 = w // half
    w0 = w % 2
    wm = w - w2 * half - w0

    peers = []
    for dw2 in (1, 0):
        for da in range(groups):
            for dw0 in range(2):
                if dw2 or da or dw0:
                    peers.append(((a + da) % groups, (w2 + dw2) % 2, (w0 + dw0) % 2))

    def device(p):
        return (p[0], p[1] * half + wm + p[2])

    def slot(p):
        return (p[2] * groups + p[0]) * 2 + p[1]

    def piece(ref, p, c):
        return ref.at[p[0] * 2 + p[1], :, p[2], c]

    def held(ref, c, s):
        return ref.at[c, pl.ds(s * mid, mid)]

    me = (a, w2, w0)
    mine = slot(me)

    def forward(c, p):
        return pltpu.make_async_remote_copy(
            src_ref=piece(x_ref, p, c), dst_ref=held(buf, c, mine),
            send_sem=fs.at[c, slot(p)], recv_sem=fr.at[c, mine],
            device_id=device(p), device_id_type=MESH)

    def arriving(c, p):
        return pltpu.make_async_remote_copy(
            src_ref=piece(x_ref, p, c), dst_ref=held(buf, c, slot(p)),
            send_sem=fs.at[c, slot(p)], recv_sem=fr.at[c, slot(p)],
            device_id=device(p), device_id_type=MESH)

    def back(c, p):
        return pltpu.make_async_remote_copy(
            src_ref=held(obuf, c, slot(p)), dst_ref=piece(out_ref, me, c),
            send_sem=bs.at[c, slot(p)], recv_sem=br.at[c, mine],
            device_id=device(p), device_id_type=MESH)

    def returning(c, p):
        return pltpu.make_async_remote_copy(
            src_ref=held(obuf, c, slot(p)), dst_ref=piece(out_ref, p, c),
            send_sem=bs.at[c, slot(p)], recv_sem=br.at[c, slot(p)],
            device_id=device(p), device_id_type=MESH)

    across = (a, (w2 + 1) % 2, w0)
    steps = [(a, w2, (w0 + 1) % 2)]
    stride = 1
    while stride < groups:
        steps.append((a + stride * (1 - 2 * ((a // stride) % 2)), w2, w0))
        stride *= 2

    barrier = pltpu.get_barrier_semaphore()
    for p in [across] + steps:
        pl.semaphore_signal(barrier, inc=1, device_id=device(p), device_id_type=MESH)
    pl.semaphore_wait(barrier, 1 + len(steps))

    forward(0, across).start()
    for k, p in enumerate(steps):
        pl.semaphore_signal(round_sem.at[k], inc=1, device_id=device(p), device_id_type=MESH)
        pl.semaphore_wait(round_sem.at[k], 1)

    for c in range(CHUNKS):
        for p in peers[1 if c == 0 else 0:]:
            forward(c, p).start()
    fetch = [pltpu.make_async_copy(order_hbm, order_ref, load.at[0]),
             pltpu.make_async_copy(bank_hbm, bank_ref, load.at[1])]
    stay = [pltpu.make_async_copy(piece(x_ref, me, c), held(buf, c, mine), own.at[0, c])
            for c in range(CHUNKS)]
    for copy in fetch + stay:
        copy.start()
    for copy in fetch:
        copy.wait()

    gates = [bank_ref[order_ref[k]] for k in range(4)]
    first = embed(gates[0][0], gates[0][1])
    third = embed(gates[2][0], gates[2][1])
    lanes_gate[...] = dot(third, first)
    real, imag = 0.0, 0.0
    for high in range(2):
        spread = spread_rows(groups, mid, gate_rows, high)
        real += dot_t(dot(spread, gates[3][0]), spread)
        imag += dot_t(dot(spread, gates[3][1]), spread)
    zero = jnp.zeros((gate_rows, gate_rows), jnp.float32)
    halves = []
    for part in range(2):
        g = gates[1][part]
        halves.append(jnp.concatenate([
            jnp.concatenate([g, zero], axis=1), jnp.concatenate([zero, g], axis=1)], axis=0))
    both = dot(embed(real, imag), jnp.concatenate(halves, axis=0))
    rows_gate[:, :rows] = both
    rows_gate[:rows, rows:] = -both[rows:]
    rows_gate[rows:, rows:] = both[:rows]

    for c in range(CHUNKS):
        for p in peers:
            arriving(c, p).wait_recv()
        stay[c].wait()
        flat_in = buf.at[c].reshape(rows * SUB, buf.shape[-1])
        flat_out = obuf.at[c].reshape(rows * SUB, buf.shape[-1])
        for q in range(SUB // 2):
            re = flat_in[pl.ds(2 * q, rows, SUB), :]
            im = flat_in[pl.ds(2 * q + 1, rows, SUB), :]
            mixed = dot_t(jnp.concatenate([re, im], axis=1), lanes_gate[...])
            tall = jnp.concatenate([mixed[:, :gate_rows], mixed[:, gate_rows:]], axis=0)
            done = dot(rows_gate[...], tall)
            flat_out[pl.ds(2 * q, rows, SUB), :] = done[:rows]
            flat_out[pl.ds(2 * q + 1, rows, SUB), :] = done[rows:]
        for p in peers if c + 1 < CHUNKS else peers[::-1]:
            back(c, p).start()
        pltpu.make_async_copy(held(obuf, c, mine), piece(out_ref, me, c), own.at[1, c]).start()

    for c in range(CHUNKS):
        for p in peers:
            returning(c, p).wait_recv()
        pltpu.make_async_copy(held(obuf, c, mine), piece(out_ref, me, c), own.at[1, c]).wait()
    for c in range(CHUNKS):
        for p in peers:
            forward(c, p).wait_send()
            back(c, p).wait_send()


def per_device(groups, wa_count, state, gate_bank, pass_order):
    lanes = gate_bank.shape[2]
    mid = lanes // (2 * groups)
    size = state.shape[1]
    shape = (2 * groups, mid, 2, CHUNKS, SUB, lanes)
    x = state.reshape(2, size // lanes, lanes).transpose(1, 0, 2).reshape(shape)
    slots = 4 * groups
    out = pl.pallas_call(
        functools.partial(kernel, groups, wa_count, mid),
        out_shape=pltpu.VMEM(shape, jnp.float32),
        in_specs=[
            pl.BlockSpec(memory_space=pl.ANY),
            pl.BlockSpec(memory_space=pl.ANY),
            pl.BlockSpec(memory_space=pl.ANY),
        ],
        out_specs=pl.BlockSpec(memory_space=pltpu.VMEM),
        scratch_shapes=[
            pltpu.SMEM(pass_order.shape, jnp.int32),
            pltpu.VMEM(gate_bank.shape, jnp.float32),
            pltpu.VMEM((2 * lanes, 2 * lanes), jnp.float32),
            pltpu.VMEM((4 * lanes, 4 * lanes), jnp.float32),
            pltpu.VMEM((CHUNKS, 2 * lanes, SUB, lanes), jnp.float32),
            pltpu.VMEM((CHUNKS, 2 * lanes, SUB, lanes), jnp.float32),
            pltpu.SemaphoreType.DMA((CHUNKS, slots)),
            pltpu.SemaphoreType.DMA((CHUNKS, slots)),
            pltpu.SemaphoreType.DMA((CHUNKS, slots)),
            pltpu.SemaphoreType.DMA((CHUNKS, slots)),
            pltpu.SemaphoreType.DMA((2, CHUNKS)),
            pltpu.SemaphoreType.DMA((2,)),
            pltpu.SemaphoreType.REGULAR((groups.bit_length(),)),
        ],
        compiler_params=pltpu.CompilerParams(collective_id=0, has_side_effects=True),
    )(pass_order, gate_bank, x)
    return out.reshape(size // lanes, 2, lanes).transpose(1, 0, 2).reshape(2, size)


def solution(mesh):
    in_specs = (P(None, ("pb", "wa")), P(), P())
    out_specs = P(None, ("pb", "wa"))
    return jax.shard_map(
        functools.partial(per_device, mesh.shape["pb"], mesh.shape["wa"]),
        mesh=mesh, in_specs=in_specs, out_specs=out_specs, check_vma=False,
    )
```

```python
import functools

import jax
import jax.numpy as jnp
from jax import lax
from jax.experimental import pallas as pl
from jax.experimental.pallas import tpu as pltpu
from jax.sharding import PartitionSpec as P

MESH = pl.DeviceIdType.MESH
HIGH = lax.Precision.HIGHEST
CHUNKS = 2
SUB = 8


def dot(a, b):
    return lax.dot_general(
        a, b, (((1,), (0,)), ((), ())), precision=HIGH, preferred_element_type=jnp.float32
    )


def dot_t(a, b):
    return lax.dot_general(
        a, b, (((1,), (1,)), ((), ())), precision=HIGH, preferred_element_type=jnp.float32
    )


def embed(real, imag):
    upper = jnp.concatenate([real, -imag], axis=1)
    lower = jnp.concatenate([imag, real], axis=1)
    return jnp.concatenate([upper, lower], axis=0)


def spread_rows(groups, mid, gate_rows, high):
    slot = lax.broadcasted_iota(jnp.int32, (2 * gate_rows, gate_rows), 0)
    row = lax.broadcasted_iota(jnp.int32, (2 * gate_rows, gate_rows), 1)
    a = row // (2 * mid)
    w0 = (row // mid) % 2
    m = row % mid
    return jnp.where(slot == ((w0 * groups + a) * 2 + high) * mid + m, 1.0, 0.0).astype(jnp.float32)


def kernel(groups, wa_count, mid, order_hbm, bank_hbm, x_ref, out_ref, order_ref, bank_ref,
           lanes_gate, rows_gate, buf, obuf, fs, fr, bs, br, own, load, round_sem):
    gate_rows = bank_ref.shape[2]
    rows = 2 * gate_rows
    a = lax.axis_index("pb")
    w = lax.axis_index("wa")
    half = wa_count // 2
    w2 = w // half
    w0 = w % 2
    wm = w - w2 * half - w0

    peers = []
    for dw2 in (1, 0):
        for da in range(groups):
            for dw0 in range(2):
                if dw2 or da or dw0:
                    peers.append(((a + da) % groups, (w2 + dw2) % 2, (w0 + dw0) % 2))

    def device(p):
        return (p[0], p[1] * half + wm + p[2])

    def slot(p):
        return (p[2] * groups + p[0]) * 2 + p[1]

    def piece(ref, p, c):
        return ref.at[p[0] * 2 + p[1], :, p[2], c]

    def held(ref, c, s):
        return ref.at[c, pl.ds(s * mid, mid)]

    me = (a, w2, w0)
    mine = slot(me)

    def forward(c, p):
        return pltpu.make_async_remote_copy(
            src_ref=piece(x_ref, p, c), dst_ref=held(buf, c, mine),
            send_sem=fs.at[c, slot(p)], recv_sem=fr.at[c, mine],
            device_id=device(p), device_id_type=MESH)

    def arriving(c, p):
        return pltpu.make_async_remote_copy(
            src_ref=piece(x_ref, p, c), dst_ref=held(buf, c, slot(p)),
            send_sem=fs.at[c, slot(p)], recv_sem=fr.at[c, slot(p)],
            device_id=device(p), device_id_type=MESH)

    def back(c, p):
        return pltpu.make_async_remote_copy(
            src_ref=held(obuf, c, slot(p)), dst_ref=piece(out_ref, me, c),
            send_sem=bs.at[c, slot(p)], recv_sem=br.at[c, mine],
            device_id=device(p), device_id_type=MESH)

    def returning(c, p):
        return pltpu.make_async_remote_copy(
            src_ref=held(obuf, c, slot(p)), dst_ref=piece(out_ref, p, c),
            send_sem=bs.at[c, slot(p)], recv_sem=br.at[c, slot(p)],
            device_id=device(p), device_id_type=MESH)

    across = (a, (w2 + 1) % 2, w0)
    steps = [(a, w2, (w0 + 1) % 2)]
    stride = 1
    while stride < groups:
        steps.append((a + stride * (1 - 2 * ((a // stride) % 2)), w2, w0))
        stride *= 2

    barrier = pltpu.get_barrier_semaphore()
    for p in [across] + steps:
        pl.semaphore_signal(barrier, inc=1, device_id=device(p), device_id_type=MESH)
    pl.semaphore_wait(barrier, 1 + len(steps))

    for c in range(CHUNKS):
        forward(c, across).start()
    for k, p in enumerate(steps):
        pl.semaphore_signal(round_sem.at[k], inc=1, device_id=device(p), device_id_type=MESH)
        pl.semaphore_wait(round_sem.at[k], 1)

    for c in range(CHUNKS):
        for p in peers[1:]:
            forward(c, p).start()
    fetch = [pltpu.make_async_copy(order_hbm, order_ref, load.at[0]),
             pltpu.make_async_copy(bank_hbm, bank_ref, load.at[1])]
    stay = [pltpu.make_async_copy(piece(x_ref, me, c), held(buf, c, mine), own.at[0, c])
            for c in range(CHUNKS)]
    for copy in fetch + stay:
        copy.start()
    for copy in fetch:
        copy.wait()

    gates = [bank_ref[order_ref[k]] for k in range(4)]
    first = embed(gates[0][0], gates[0][1])
    third = embed(gates[2][0], gates[2][1])
    lanes_gate[...] = dot(third, first)
    real, imag = 0.0, 0.0
    for high in range(2):
        spread = spread_rows(groups, mid, gate_rows, high)
        real += dot_t(dot(spread, gates[3][0]), spread)
        imag += dot_t(dot(spread, gates[3][1]), spread)
    zero = jnp.zeros((gate_rows, gate_rows), jnp.float32)
    halves = []
    for part in range(2):
        g = gates[1][part]
        halves.append(jnp.concatenate([
            jnp.concatenate([g, zero], axis=1), jnp.concatenate([zero, g], axis=1)], axis=0))
    both = dot(embed(real, imag), jnp.concatenate(halves, axis=0))
    rows_gate[:, :rows] = both
    rows_gate[:rows, rows:] = -both[rows:]
    rows_gate[rows:, rows:] = both[:rows]

    for c in range(CHUNKS):
        for p in peers:
            arriving(c, p).wait_recv()
        stay[c].wait()
        flat_in = buf.at[c].reshape(rows * SUB, buf.shape[-1])
        flat_out = obuf.at[c].reshape(rows * SUB, buf.shape[-1])
        for q in range(SUB // 2):
            re = flat_in[pl.ds(2 * q, rows, SUB), :]
            im = flat_in[pl.ds(2 * q + 1, rows, SUB), :]
            mixed = dot_t(jnp.concatenate([re, im], axis=1), lanes_gate[...])
            tall = jnp.concatenate([mixed[:, :gate_rows], mixed[:, gate_rows:]], axis=0)
            done = dot(rows_gate[...], tall)
            flat_out[pl.ds(2 * q, rows, SUB), :] = done[:rows]
            flat_out[pl.ds(2 * q + 1, rows, SUB), :] = done[rows:]
        for p in peers if c + 1 < CHUNKS else peers[::-1]:
            back(c, p).start()
        pltpu.make_async_copy(held(obuf, c, mine), piece(out_ref, me, c), own.at[1, c]).start()

    for c in range(CHUNKS):
        for p in peers:
            returning(c, p).wait_recv()
        pltpu.make_async_copy(held(obuf, c, mine), piece(out_ref, me, c), own.at[1, c]).wait()
    for c in range(CHUNKS):
        for p in peers:
            forward(c, p).wait_send()
            back(c, p).wait_send()


def per_device(groups, wa_count, state, gate_bank, pass_order):
    lanes = gate_bank.shape[2]
    mid = lanes // (2 * groups)
    size = state.shape[1]
    shape = (2 * groups, mid, 2, CHUNKS, SUB, lanes)
    x = state.reshape(2, size // lanes, lanes).transpose(1, 0, 2).reshape(shape)
    slots = 4 * groups
    out = pl.pallas_call(
        functools.partial(kernel, groups, wa_count, mid),
        out_shape=pltpu.VMEM(shape, jnp.float32),
        in_specs=[
            pl.BlockSpec(memory_space=pl.ANY),
            pl.BlockSpec(memory_space=pl.ANY),
            pl.BlockSpec(memory_space=pl.ANY),
        ],
        out_specs=pl.BlockSpec(memory_space=pltpu.VMEM),
        scratch_shapes=[
            pltpu.SMEM(pass_order.shape, jnp.int32),
            pltpu.VMEM(gate_bank.shape, jnp.float32),
            pltpu.VMEM((2 * lanes, 2 * lanes), jnp.float32),
            pltpu.VMEM((4 * lanes, 4 * lanes), jnp.float32),
            pltpu.VMEM((CHUNKS, 2 * lanes, SUB, lanes), jnp.float32),
            pltpu.VMEM((CHUNKS, 2 * lanes, SUB, lanes), jnp.float32),
            pltpu.SemaphoreType.DMA((CHUNKS, slots)),
            pltpu.SemaphoreType.DMA((CHUNKS, slots)),
            pltpu.SemaphoreType.DMA((CHUNKS, slots)),
            pltpu.SemaphoreType.DMA((CHUNKS, slots)),
            pltpu.SemaphoreType.DMA((2, CHUNKS)),
            pltpu.SemaphoreType.DMA((2,)),
            pltpu.SemaphoreType.REGULAR((groups.bit_length(),)),
        ],
        compiler_params=pltpu.CompilerParams(collective_id=0, has_side_effects=True),
    )(pass_order, gate_bank, x)
    return out.reshape(size // lanes, 2, lanes).transpose(1, 0, 2).reshape(2, size)


def solution(mesh):
    in_specs = (P(None, ("pb", "wa")), P(), P())
    out_specs = P(None, ("pb", "wa"))
    return jax.shard_map(
        functools.partial(per_device, mesh.shape["pb"], mesh.shape["wa"]),
        mesh=mesh, in_specs=in_specs, out_specs=out_specs, check_vma=False,
    )
```
